32 devices in a mesh: groups: 2 (over x), seq: 16 (over z, y, core).
Axes of the slice: x: 2, y: 2, z: 4, core: 2. Of those that a mesh axis runs over, the one named last changes fastest.
Arguments:
- tokens: bfloat16 [16384, 1024], P(('groups', 'seq')), parts along dimension 0, may hold values from -32 to 32
- w_query: bfloat16 [1024, 1024], replicated, may hold values from -0.1875 to 0.1875
- w_key: bfloat16 [1024, 1024], replicated, may hold values from -0.1875 to 0.1875
- w_value: bfloat16 [1024, 1024], replicated, may hold values from -0.1875 to 0.1875
- w_out: bfloat16 [1024, 1024], replicated, may hold values from -0.1875 to 0.1875
- rand_table: int32 [128, 3], replicated, may hold values from 0 to 127, as said below
- global_blocks: int32 [2], replicated, may hold values from 0 to 127
Outputs:
- attended: bfloat16 [16384, 1024], P(('groups', 'seq')), parts along dimension 0
The draws below stay inside these ranges and needn't reach their ends.
There are 2 independent parts, one for each index of `groups`. The reference program is written for one: setup_inputs(seed, part) draws one part's arguments, and reference() takes and returns one part's arrays. A program takes and returns all parts, laid end to end along the dimension named above; an argument that names none is the same for every part. Nothing has to cross between parts.
Inputs may be any that keep to these rules, and one draw needn't show every extreme that they name: `rand_table`: block j of the document lies on index j // 8 of seq. Among the 24 entries of the query blocks of one device, at most 3 name blocks of any one device, and some device is named exactly 3 times by the entries of every device.
All inputs are finite; a program needn't handle non-finite values.
Results may differ from the reference program's by a relative error of at most 0.01.
The reference program's roundings to bfloat16 on the way (of `weights`, `sparse` and `mixed`) count: a program that leaves them out, or rounds other values in their place, can miss the bound.
Values may be sent and summed in bfloat16 or wider, within the bound.
No kernel may reach another device: no remote copies, remote signals or barrier semaphores. Data moves between devices by JAX's collectives and lax.ppermute only.
A program may use at most 192 MiB of HBM per device.

```python
import math
import jax
import jax.numpy as jnp
from jax import lax

D = 1024
HEADS = 16
BLOCK = 64
BLOCKS_DEV = 8
NBLK = 128
TOKENS = 8192
CAP = 3


def draw_tokens(key, part):
    return jnp.clip(jax.random.normal(key, (TOKENS, D), jnp.float32), -6.0, 6.0).astype(jnp.bfloat16)


def draw_rand_table(key, part):
    devices = NBLK // BLOCKS_DEV
    slots = 3 * BLOCKS_DEV
    tokens_all = devices * CAP
    hot_key, rest_key = jax.random.split(jax.random.fold_in(key, 7))
    order = jax.random.permutation(hot_key, devices)
    is_hot = jnp.zeros((devices,), jnp.int32).at[order[:2]].set(1)
    token_owner = jnp.repeat(jnp.arange(devices, dtype=jnp.int32), CAP, total_repeat_length=tokens_all)
    token_copy = jnp.tile(jnp.arange(CAP, dtype=jnp.int32), devices)

    def one_receiver(receiver):
        receiver_key = jax.random.fold_in(rest_key, receiver)
        noise_key, local_key, shuffle_key = jax.random.split(receiver_key, 3)
        noise = jax.random.randint(noise_key, (tokens_all,), 0, 1 << 16)
        score = jnp.where(is_hot[token_owner] == 1, token_copy, CAP + noise)
        score = score * tokens_all + jnp.arange(tokens_all, dtype=jnp.int32)
        picked = jnp.argsort(score)[:slots]
        owners = token_owner[picked]
        owners = owners[jax.random.permutation(shuffle_key, slots)]
        local = jax.random.randint(local_key, (slots,), 0, BLOCKS_DEV)
        return (owners * BLOCKS_DEV + local).astype(jnp.int32)
    table = jax.vmap(one_receiver)(jnp.arange(devices, dtype=jnp.int32))
    return table.reshape(NBLK, 3)


def bell_draw(own_key, extent, deviation, reach, kind=jnp.bfloat16):
    entries = deviation * jax.random.normal(own_key, extent, jnp.float32)
    return jnp.clip(entries, min=-reach, max=reach).astype(kind)


def setup_inputs(seed: int = 0, part: int = 0) -> dict:
    splits = jax.random.split(jax.random.key(seed), 8)
    part_splits = jax.random.split(jax.random.fold_in(splits[7], part), 8)
    tokens = draw_tokens(jax.random.fold_in(jax.random.fold_in(splits[7], part), 71), part)
    w_query = bell_draw(splits[1], (D, D), D ** -0.5, 0.1875)
    w_key = bell_draw(splits[2], (D, D), D ** -0.5, 0.1875)
    w_value = bell_draw(splits[3], (D, D), D ** -0.5, 0.1875)
    w_out = bell_draw(splits[4], (D, D), D ** -0.5, 0.1875)
    rand_table = draw_rand_table(jax.random.fold_in(splits[7], 71), part)
    global_blocks = jax.random.randint(splits[6], (2,), 0, NBLK).astype(jnp.int32)
    return dict(tokens=tokens, w_query=w_query, w_key=w_key, w_value=w_value, w_out=w_out, rand_table=rand_table, global_blocks=global_blocks)


def reference(tokens, w_query, w_key, w_value, w_out, rand_table, global_blocks):
    width = tokens.shape[1]
    head_dim = width // HEADS
    scale = 1.0 / math.sqrt(head_dim)
    queries = jnp.dot(tokens, w_query, preferred_element_type=jnp.float32).astype(jnp.bfloat16)
    keys = jnp.dot(tokens, w_key, preferred_element_type=jnp.float32).astype(jnp.bfloat16)
    values = jnp.dot(tokens, w_value, preferred_element_type=jnp.float32).astype(jnp.bfloat16)
    query_blocks = queries.reshape(NBLK, BLOCK, width)
    key_blocks = keys.reshape(NBLK, BLOCK, width)
    value_blocks = values.reshape(NBLK, BLOCK, width)
    block_ids = jnp.arange(NBLK, dtype=jnp.int32)
    window = jnp.stack([(block_ids - 1) % NBLK, block_ids, (block_ids + 1) % NBLK], axis=1).astype(jnp.int32)
    shared = jnp.broadcast_to(global_blocks[None, :], (NBLK, 2)).astype(jnp.int32)
    listed = jnp.concatenate([window, rand_table.astype(jnp.int32), shared], axis=1)
    group = math.gcd(NBLK, 8)

    def one_group(start):
        index = start * group + jnp.arange(group, dtype=jnp.int32)
        chosen = listed[index]
        picked_keys = key_blocks[chosen].reshape(group, 8 * BLOCK, HEADS, head_dim).astype(jnp.float32)
        picked_values = value_blocks[chosen].reshape(group, 8 * BLOCK, HEADS, head_dim).astype(jnp.float32)
        block_queries = query_blocks[index].reshape(group, BLOCK, HEADS, head_dim).astype(jnp.float32)
        scores = jnp.einsum('gqhd,gkhd->ghqk', block_queries, picked_keys, precision=lax.Precision.HIGHEST) * scale
        weights = jax.nn.softmax(scores, axis=-1).astype(jnp.bfloat16).astype(jnp.float32)
        mixed = jnp.einsum('ghqk,gkhd->gqhd', weights, picked_values, precision=lax.Precision.HIGHEST)
        return mixed.astype(jnp.bfloat16).reshape(group, BLOCK, width)
    sparse = lax.map(one_group, jnp.arange(NBLK // group, dtype=jnp.int32)).reshape(NBLK, BLOCK, width)
    global_query = query_blocks[global_blocks].reshape(2 * BLOCK, HEADS, head_dim).astype(jnp.float32)
    all_keys = keys.reshape(TOKENS, HEADS, head_dim).astype(jnp.float32)
    all_values = values.reshape(TOKENS, HEADS, head_dim).astype(jnp.float32)
    full_scores = jnp.einsum('qhd,khd->qhk', global_query, all_keys, precision=lax.Precision.HIGHEST) * scale
    full_weights = jax.nn.softmax(full_scores, axis=-1)
    full_out = jnp.einsum('qhk,khd->qhd', full_weights, all_values, precision=lax.Precision.HIGHEST)
    full_out = full_out.astype(jnp.bfloat16).reshape(2, BLOCK, width)
    mixed = sparse.at[global_blocks].set(full_out).reshape(TOKENS, width)
    return jnp.dot(mixed, w_out, preferred_element_type=jnp.float32).astype(jnp.bfloat16)
```

```python
import math

import jax
import jax.numpy as jnp
from jax import lax
from jax.experimental import pallas as pl
from jax.experimental.pallas import tpu as pltpu
from jax.sharding import PartitionSpec as P

HEADS = 16
BLOCK = 64
GROUP = 4
NT = (((1,), (1,)), ((), ()))
BF16 = jnp.bfloat16
F32 = jnp.float32


def lane_head(shape, head_dim):
    return lax.broadcasted_iota(jnp.int32, shape, 1) // head_dim


def spread_heads(q, head_dim):
    which = lane_head(q.shape, head_dim)
    zero = jnp.zeros_like(q)
    return jnp.concatenate([jnp.where(which == j, q, zero) for j in range(GROUP)], axis=0)


def fold_heads(wide, head_dim):
    rows = wide.shape[0] // GROUP
    which = lane_head((rows, wide.shape[1]), head_dim)
    out = wide[:rows]
    for j in range(1, GROUP):
        out = jnp.where(which == j, wide[j * rows : (j + 1) * rows], out)
    return out


def project_kernel(ids, tokens, w_key, w_value, out, rows, sem):
    count = rows.shape[0] // BLOCK

    def copy(i):
        start = pl.multiple_of(ids[i] * BLOCK, BLOCK)
        return pltpu.make_async_copy(
            tokens.at[pl.ds(start, BLOCK), :], rows.at[pl.ds(i * BLOCK, BLOCK), :], sem.at[i]
        )

    for i in range(count):
        copy(i).start()
    width = w_key.shape[1]
    chunk = 8
    for first in range(0, count, chunk):
        last = min(first + chunk, count)
        for i in range(first, last):
            copy(i).wait()
        span = slice(first * BLOCK, last * BLOCK)
        out[span, :width] = jnp.dot(rows[span, :], w_key[...], preferred_element_type=F32).astype(BF16)
        out[span, width:] = jnp.dot(rows[span, :], w_value[...], preferred_element_type=F32).astype(BF16)


def attend_kernel(
    pos, own, queries, keys, values, global_kv, other_kv, w_out, fixed, out, kbuf, vbuf, mixed, sem
):
    rows, width = queries.shape
    head_dim = width // HEADS
    blocks = rows // BLOCK
    lanes = GROUP * head_dim
    g_rows = global_kv.shape[0]
    o_rows = other_kv.shape[0]
    copies = [
        pltpu.make_async_copy(keys, kbuf.at[pl.ds(0, rows), :], sem.at[0]),
        pltpu.make_async_copy(values, vbuf.at[pl.ds(0, rows), :], sem.at[1]),
        pltpu.make_async_copy(global_kv.at[:, pl.ds(0, width)], kbuf.at[pl.ds(rows, g_rows), :], sem.at[2]),
        pltpu.make_async_copy(global_kv.at[:, pl.ds(width, width)], vbuf.at[pl.ds(rows, g_rows), :], sem.at[3]),
        pltpu.make_async_copy(other_kv.at[:, pl.ds(0, width)], kbuf.at[pl.ds(rows + g_rows, o_rows), :], sem.at[4]),
        pltpu.make_async_copy(other_kv.at[:, pl.ds(width, width)], vbuf.at[pl.ds(rows + g_rows, o_rows), :], sem.at[5]),
    ]
    for c in copies:
        c.start()
    for c in copies:
        c.wait()

    def one_block(i, carry):
        here = pl.ds(pl.multiple_of(i * BLOCK, BLOCK), BLOCK)
        places = [pl.ds(pl.multiple_of(pos[i * 8 + t] * BLOCK, BLOCK), BLOCK) for t in range(8)]
        for g in range(HEADS // GROUP):
            cols = slice(g * lanes, (g + 1) * lanes)
            q = spread_heads(queries[here, cols], head_dim)
            k = jnp.concatenate([kbuf[p, cols] for p in places], axis=0)
            v = jnp.concatenate([vbuf[p, cols] for p in places], axis=0)
            scores = lax.dot_general(q, k, NT, preferred_element_type=F32)
            top = jnp.max(scores, axis=1, keepdims=True)
            expo = jnp.exp(scores - top)
            total = jnp.sum(expo, axis=1, keepdims=True)
            weights = (expo * (1.0 / total)).astype(BF16)
            wide = jnp.dot(weights, v, preferred_element_type=F32)
            mixed[here, cols] = fold_heads(wide, head_dim).astype(BF16)
        return carry

    lax.fori_loop(0, blocks, one_block, 0)
    out[...] = jnp.dot(mixed[...], w_out[...], preferred_element_type=F32).astype(BF16)
    for j in range(2):

        @pl.when(own[2 * j] == 1)
        def _():
            out[pl.ds(pl.multiple_of(own[2 * j + 1] * BLOCK, BLOCK), BLOCK), :] = fixed[
                j * BLOCK : (j + 1) * BLOCK, :
            ]


def global_kernel(queries, keys, values, out):
    width = queries.shape[1]
    head_dim = width // HEADS
    lanes = GROUP * head_dim
    lane = lax.broadcasted_iota(jnp.int32, (BLOCK, 128), 1)
    for b in range(queries.shape[0] // BLOCK):
        here = slice(b * BLOCK, (b + 1) * BLOCK)
        tops = jnp.zeros((BLOCK, 128), F32)
        totals = jnp.zeros((BLOCK, 128), F32)
        for g in range(HEADS // GROUP):
            cols = slice(g * lanes, (g + 1) * lanes)
            q = spread_heads(queries[here, cols], head_dim)
            scores = lax.dot_general(q, keys[:, cols], NT, preferred_element_type=F32)
            top = jnp.max(scores, axis=1, keepdims=True)
            expo = jnp.exp(scores - top)
            total = jnp.sum(expo, axis=1, keepdims=True)
            high = expo.astype(BF16)
            low = (expo - high.astype(F32)).astype(BF16)
            v = values[:, cols]
            wide = jnp.dot(high, v, preferred_element_type=F32) + jnp.dot(low, v, preferred_element_type=F32)
            out[here, cols] = fold_heads(wide, head_dim)
            for j in range(GROUP):
                mine = lane == g * GROUP + j
                part = slice(j * BLOCK, (j + 1) * BLOCK)
                tops = jnp.where(mine, top[part], tops)
                totals = jnp.where(mine, total[part], totals)
        out[here, width : width + 128] = tops
        out[here, width + 128 : width + 256] = totals


def whole(memory=pltpu.VMEM):
    return pl.BlockSpec(memory_space=memory)


def swap(array, axis, bit):
    count = lax.axis_size(axis)
    return lax.ppermute(array, axis, [(i, i ^ bit) for i in range(count)])


def on_device(tokens, w_query, w_key, w_value, w_out, rand_table, global_blocks):
    rows, width = tokens.shape
    head_dim = width // HEADS
    blocks = rows // BLOCK
    devices = lax.axis_size("seq")
    total_blocks = devices * blocks
    myself = lax.axis_index("seq")
    scale = 1.0 / math.sqrt(head_dim)
    limit = pltpu.CompilerParams(vmem_limit_bytes=56 << 20)

    everything = lax.all_gather(tokens, "seq", tiled=True)

    owner = global_blocks // blocks
    local = global_blocks % blocks
    owned = owner == myself
    mine = tokens.reshape(blocks, BLOCK, width)
    global_tokens = jnp.concatenate(
        [
            jnp.where(owned[j], lax.dynamic_index_in_dim(mine, local[j], 0, keepdims=False), jnp.zeros((), BF16))
            for j in range(2)
        ],
        axis=0,
    )
    bit = 1
    while bit < devices:
        global_tokens = global_tokens + swap(global_tokens, "seq", bit)
        bit *= 2

    def project(array, weight):
        return jnp.dot(array, weight, preferred_element_type=F32).astype(BF16)

    queries = project(tokens, w_query) * jnp.asarray(scale, BF16)
    keys = project(tokens, w_key)
    values = project(tokens, w_value)
    global_queries = project(global_tokens, w_query) * jnp.asarray(scale, BF16)
    global_kv = jnp.concatenate([project(global_tokens, w_key), project(global_tokens, w_value)], axis=1)

    g_rows = 2 * BLOCK
    payload = width + 256
    partial = pl.pallas_call(
        global_kernel,
        out_shape=jax.ShapeDtypeStruct((g_rows, payload), F32),
        in_specs=[whole()] * 3,
        out_specs=whole(),
        compiler_params=limit,
    )(global_queries, keys, values)
    share = g_rows // devices
    parts = lax.all_to_all(partial, "seq", 0, 0, tiled=True).reshape(devices, share, payload)
    tops = parts[:, :, width : width + HEADS]
    totals = parts[:, :, width + 128 : width + 128 + HEADS]
    factor = jnp.exp(tops - jnp.max(tops, axis=0, keepdims=True))
    factor = factor / jnp.sum(factor * totals, axis=0, keepdims=True)
    expand = (jnp.arange(width)[None, :] // head_dim == jnp.arange(HEADS)[:, None]).astype(F32)
    factor = jnp.dot(factor.reshape(devices * share, HEADS), expand, precision=lax.Precision.HIGHEST)
    full = jnp.sum(parts[:, :, :width] * factor.reshape(devices, share, width), axis=0).astype(BF16)
    fixed = project(full, w_out)
    bit = 1
    while bit < devices:
        theirs = swap(fixed, "seq", bit)
        upper = (myself // bit) % 2 == 1
        fixed = jnp.concatenate([jnp.where(upper, theirs, fixed), jnp.where(upper, fixed, theirs)], axis=0)
        bit *= 2

    first = myself * blocks
    slots = lax.dynamic_slice_in_dim(rand_table, first, blocks, 0).reshape(3 * blocks)
    edges = jnp.stack([(first - 1) % total_blocks, (first + blocks) % total_blocks])
    wanted = jnp.concatenate([edges, slots]).astype(jnp.int32)
    count = 3 * blocks + 2
    other_kv = pl.pallas_call(
        project_kernel,
        out_shape=jax.ShapeDtypeStruct((count * BLOCK, 2 * width), BF16),
        in_specs=[whole(pltpu.SMEM), whole(pl.ANY), whole(), whole()],
        out_specs=whole(),
        scratch_shapes=[pltpu.VMEM((count * BLOCK, width), BF16), pltpu.SemaphoreType.DMA((count,))],
        compiler_params=limit,
    )(wanted, everything, w_key, w_value)

    place = []
    for i in range(blocks):
        before = i - 1 if i > 0 else blocks + 2
        after = i + 1 if i + 1 < blocks else blocks + 3
        rand = [blocks + 4 + 3 * i + t for t in range(3)]
        place += [before, i, after] + rand + [blocks, blocks + 1]
    place = jnp.array(place, jnp.int32)
    own = jnp.stack([owned.astype(jnp.int32), local.astype(jnp.int32)], axis=1).reshape(4)
    held = rows + g_rows + count * BLOCK
    return pl.pallas_call(
        attend_kernel,
        out_shape=jax.ShapeDtypeStruct((rows, width), BF16),
        in_specs=[whole(pltpu.SMEM), whole(pltpu.SMEM), whole()]
        + [whole(pl.ANY)] * 4
        + [whole(), whole()],
        out_specs=whole(),
        scratch_shapes=[
            pltpu.VMEM((held, width), BF16),
            pltpu.VMEM((held, width), BF16),
            pltpu.VMEM((rows, width), BF16),
            pltpu.SemaphoreType.DMA((6,)),
        ],
        compiler_params=limit,
    )(place, own, queries, keys, values, global_kv, other_kv, w_out, fixed)


def solution(mesh):
    in_specs = (P(("groups", "seq"), None), P(), P(), P(), P(), P(), P())
    out_specs = P(("groups", "seq"), None)
    return jax.shard_map(
        on_device, mesh=mesh, in_specs=in_specs, out_specs=out_specs, check_vma=False
    )
```

```python
import math

import jax
import jax.numpy as jnp
from jax import lax
from jax.experimental import pallas as pl
from jax.experimental.pallas import tpu as pltpu
from jax.sharding import PartitionSpec as P

HEADS = 16
BLOCK = 64
GROUP = 4
CHUNK = 4
NT = (((1,), (1,)), ((), ()))
BF16 = jnp.bfloat16
F32 = jnp.float32


def in_hbm(*arrays):
    return [pltpu.with_memory_space_constraint(a, pltpu.HBM) for a in arrays]


def hbm_out(shape, dtype):
    return pltpu.HBM(shape, dtype)


def whole(memory=pltpu.VMEM):
    return pl.BlockSpec(memory_space=memory)


def rows_at(block, count=1):
    return pl.ds(pl.multiple_of(block * BLOCK, BLOCK), count * BLOCK)


def lane_head(shape, head_dim):
    return lax.broadcasted_iota(jnp.int32, shape, 1) // head_dim


def spread_heads(q, head_dim):
    which = lane_head(q.shape, head_dim)
    zero = jnp.zeros_like(q)
    return jnp.concatenate([jnp.where(which == j, q, zero) for j in range(GROUP)], axis=0)


def fold_heads(wide, head_dim):
    rows = wide.shape[0] // GROUP
    which = lane_head((rows, wide.shape[1]), head_dim)
    out = wide[:rows]
    for j in range(1, GROUP):
        out = jnp.where(which == j, wide[j * rows : (j + 1) * rows], out)
    return out


class Layout:
    def __init__(self, devices, blocks):
        self.devices, self.blocks = devices, blocks
        self.tall = devices // 4
        self.slots = 3 * blocks
        self.caps = -(-self.slots // devices) + 1
        self.asked = 0
        self.bounds = self.asked + self.tall * 3 * self.caps
        self.order = self.bounds + self.tall + 2
        self.source = self.order + self.slots
        self.index = self.source + self.slots
        self.own = self.index + self.slots
        self.core = self.own + 4
        self.spare = self.core + 1
        self.size = self.spare + 1


def make_route(lay):
    devices, blocks, tall, slots, caps = lay.devices, lay.blocks, lay.tall, lay.slots, lay.caps
    power = blocks.bit_length() - 1
    assert blocks == 1 << power and tall & (tall - 1) == 0

    def route_kernel(me, table, global_blocks, out, seen, stages, filled):
        myself = me[0]
        zero = jnp.int32(0)

        for i in range(tall * 3 * caps):
            out[lay.asked + i] = zero

        for t in range(1, 4):
            for w in range(tall):
                filled[w] = zero

            def asks(i, carry):
                for u in range(3):
                    block = table[(myself ^ t) * blocks + i, u]
                    apart = (block >> power) ^ myself
                    fits = (apart & 3) == 0
                    which = apart >> 2
                    rank = filled[which]
                    filled[which] = rank + fits.astype(jnp.int32)
                    at = lay.asked + (which * 3 + t - 1) * caps + rank
                    out[jnp.where(fits, at, lay.spare)] = block & (blocks - 1)
                return carry

            lax.fori_loop(0, blocks, asks, 0)

        for o in range(devices):
            seen[o] = zero
        for g in range(tall + 2):
            filled[g] = zero

        def mine(i, carry):
            for u in range(3):
                block = table[myself * blocks + i, u]
                owner = block >> power
                local = block & (blocks - 1)
                rank = seen[owner]
                seen[owner] = rank + 1
                s = i * 3 + u
                apart = owner ^ myself
                stage = 1 + (apart >> 2)
                source = apart & 3
                out[lay.source + s] = source
                out[lay.index + s] = jnp.where(source == 0, local, rank)
                stages[s] = stage
                filled[stage] = filled[stage] + 1
            return carry

        lax.fori_loop(0, blocks, mine, 0)
        start = zero
        for g in range(tall + 2):
            out[lay.bounds + g] = start
            if g < tall + 1:
                now = filled[g]
                filled[g] = start
                start = start + now

        def put(s, carry):
            stage = stages[s]
            at = filled[stage]
            filled[stage] = at + 1
            out[lay.order + at] = s
            return carry

        lax.fori_loop(0, slots, put, 0)
        for j in range(2):
            g = global_blocks[j]
            out[lay.own + 2 * j] = ((g >> power) == myself).astype(jnp.int32)
            out[lay.own + 2 * j + 1] = g & (blocks - 1)
        out[lay.core] = myself & 1
        out[lay.spare] = zero

    return pl.pallas_call(
        route_kernel,
        out_shape=jax.ShapeDtypeStruct((lay.size,), jnp.int32),
        in_specs=[whole(pltpu.SMEM)] * 3,
        out_specs=whole(pltpu.SMEM),
        scratch_shapes=[
            pltpu.SMEM((devices,), jnp.int32),
            pltpu.SMEM((slots,), jnp.int32),
            pltpu.SMEM((tall + 2,), jnp.int32),
        ],
    )


def start_all(copies):
    for c in copies:
        c.start()
    for c in copies:
        c.wait()


def owned_pair(lay, me, global_blocks, tokens):
    blocks = lay.blocks

    def kernel(me, global_blocks, tokens, pair, sem):
        start_all(
            [
                pltpu.make_async_copy(
                    tokens.at[rows_at(global_blocks[j] % blocks), :], pair.at[pl.ds(j * BLOCK, BLOCK), :], sem.at[j]
                )
                for j in range(2)
            ]
        )
        for j in range(2):

            @pl.when(global_blocks[j] // blocks != me[0])
            def _():
                pair[j * BLOCK : (j + 1) * BLOCK, :] = jnp.zeros((BLOCK, pair.shape[1]), BF16)

    return pl.pallas_call(
        kernel,
        out_shape=jax.ShapeDtypeStruct((2 * BLOCK, tokens.shape[1]), BF16),
        in_specs=[whole(pltpu.SMEM)] * 2 + [whole(pltpu.HBM)],
        out_specs=whole(),
        scratch_shapes=[pltpu.SemaphoreType.DMA((2,))],
    )(me, global_blocks, *in_hbm(tokens))


def pick(lay, which, table, tokens):
    caps = lay.caps
    base = lay.asked + which * 3 * caps

    def kernel(table, tokens, *refs):
        outs, rows, sem_in, sem_out = refs[:3], refs[3], refs[4], refs[5]
        gets = [
            pltpu.make_async_copy(
                tokens.at[rows_at(table[base + i]), :], rows.at[pl.ds(i * BLOCK, BLOCK), :], sem_in.at[i]
            )
            for i in range(3 * caps)
        ]
        puts = [
            pltpu.make_async_copy(rows.at[pl.ds(t * caps * BLOCK, caps * BLOCK), :], outs[t], sem_out.at[t])
            for t in range(3)
        ]
        for c in gets:
            c.start()
        for t in range(3):
            for c in gets[t * caps : (t + 1) * caps]:
                c.wait()
            puts[t].start()
        for c in puts:
            c.wait()

    return pl.pallas_call(
        kernel,
        out_shape=[hbm_out((caps * BLOCK, tokens.shape[1]), BF16)] * 3,
        in_specs=[whole(pltpu.SMEM), whole(pltpu.HBM)],
        out_specs=[whole(pltpu.HBM)] * 3,
        scratch_shapes=[
            pltpu.VMEM((3 * caps * BLOCK, tokens.shape[1]), BF16),
            pltpu.SemaphoreType.DMA((3 * caps,)),
            pltpu.SemaphoreType.DMA((3,)),
        ],
    )(table, *in_hbm(tokens))


def project_stages(lay, first_stage, last_stage, table, sets, w_key, w_value, kv):
    flat = [array for arrays in sets for array in arrays]

    def kernel(table, *refs):
        arrived, from_key, from_value = refs[: len(flat)], refs[len(flat)], refs[len(flat) + 1]
        out, w_key, w_value, rows, made, sem_w, sem_in, sem_out = refs[-8:]
        width = w_key.shape[1]
        loads = [
            pltpu.make_async_copy(from_key, w_key, sem_w.at[0]),
            pltpu.make_async_copy(from_value, w_value, sem_w.at[1]),
        ]
        for c in loads:
            c.start()
        low = table[lay.bounds + first_stage]
        high = table[lay.bounds + last_stage + 1]

        def one_chunk(c, carry):
            first = low + c * CHUNK

            def get(j, ref, here):
                return pltpu.make_async_copy(ref.at[here, :], rows.at[pl.ds(j * BLOCK, BLOCK), :], sem_in.at[j])

            def fetch(j):
                e = table[lay.order + first + j]
                here = rows_at(table[lay.index + e])
                source = table[lay.source + e]
                for i in range(len(sets)):
                    stage = first_stage + i
                    inside = (first + j >= table[lay.bounds + stage]) & (first + j < table[lay.bounds + stage + 1])
                    for t in range(4):

                        @pl.when(inside & (source == t))
                        def _():
                            get(j, arrived[4 * i + t], here).start()

            def put(j):
                to = rows_at(table[lay.order + first + j])
                return pltpu.make_async_copy(made.at[pl.ds(j * BLOCK, BLOCK), :], out.at[to, :], sem_out.at[j])

            def each(action):
                for j in range(CHUNK):

                    @pl.when(first + j < high)
                    def _():
                        action(j)

            each(fetch)
            each(lambda j: get(j, arrived[0], pl.ds(0, BLOCK)).wait())

            @pl.when(c == 0)
            def _():
                for load in loads:
                    load.wait()

            made[:, :width] = jnp.dot(rows[...], w_key[...], preferred_element_type=F32).astype(BF16)
            made[:, width:] = jnp.dot(rows[...], w_value[...], preferred_element_type=F32).astype(BF16)
            each(lambda j: put(j).start())
            each(lambda j: put(j).wait())
            return carry

        lax.fori_loop(0, (high - low + CHUNK - 1) // CHUNK, one_chunk, 0)

        @pl.when(high == low)
        def _():
            for load in loads:
                load.wait()

    width = w_key.shape[1]
    arrays = [table] + flat + [w_key, w_value]
    specs = [whole(pltpu.SMEM)] + [whole(pltpu.HBM)] * (len(flat) + 2)
    aliases = {}
    if kv is not None:
        aliases = {len(arrays): 0}
        arrays.append(kv)
        specs.append(whole(pltpu.HBM))
    return pl.pallas_call(
        kernel,
        out_shape=hbm_out((lay.slots * BLOCK, 2 * width), BF16),
        in_specs=specs,
        out_specs=whole(pltpu.HBM),
        scratch_shapes=[
            pltpu.VMEM((width, width), BF16),
            pltpu.VMEM((width, width), BF16),
            pltpu.VMEM((CHUNK * BLOCK, width), BF16),
            pltpu.VMEM((CHUNK * BLOCK, 2 * width), BF16),
            pltpu.SemaphoreType.DMA((2,)),
            pltpu.SemaphoreType.DMA((CHUNK,)),
            pltpu.SemaphoreType.DMA((CHUNK,)),
        ],
        input_output_aliases=aliases,
        compiler_params=pltpu.CompilerParams(vmem_limit_bytes=12 << 20),
    )(arrays[0], *in_hbm(*arrays[1:]))


def local_kernel(tokens, w_query, w_key, w_value, queries, keys, values):
    scale = jnp.asarray(1.0 / math.sqrt(queries.shape[1] // GROUP), BF16)
    x = tokens[...]
    queries[...] = jnp.dot(x, w_query[...], preferred_element_type=F32).astype(BF16) * scale
    keys[...] = jnp.dot(x, w_key[...], preferred_element_type=F32).astype(BF16)
    values[...] = jnp.dot(x, w_value[...], preferred_element_type=F32).astype(BF16)


def local_projection(tokens, weights):
    rows, width = tokens.shape
    lanes = width * GROUP // HEADS
    column = lambda g: (0, g)
    return pl.pallas_call(
        local_kernel,
        grid=(width // lanes,),
        out_shape=[hbm_out((rows, width), BF16)] * 3,
        in_specs=[pl.BlockSpec((rows, width), lambda g: (0, 0))] + [pl.BlockSpec((width, lanes), column)] * 3,
        out_specs=[pl.BlockSpec((rows, lanes), column)] * 3,
        compiler_params=pltpu.CompilerParams(vmem_limit_bytes=20 << 20),
    )(*in_hbm(tokens, *weights))


def make_near(lay):
    def near_kernel(table, half, theirs, low, high, w_query, w_key, w_value, keys, values, near_k, near_v, part, x):
        lanes = keys.shape[1]
        head_dim = lanes // GROUP
        scale = jnp.asarray(1.0 / math.sqrt(head_dim), BF16)

        @pl.when(pl.program_id(0) == 0)
        def _():
            x[2 * BLOCK : 3 * BLOCK, :] = low[...]
            x[3 * BLOCK :, :] = high[...]

            @pl.when(table[lay.core] == 0)
            def _():
                x[:BLOCK, :] = half[...]
                x[BLOCK : 2 * BLOCK, :] = theirs[...]

            @pl.when(table[lay.core] == 1)
            def _():
                x[:BLOCK, :] = theirs[...]
                x[BLOCK : 2 * BLOCK, :] = half[...]

        near_k[...] = jnp.dot(x[...], w_key[...], preferred_element_type=F32).astype(BF16)
        near_v[...] = jnp.dot(x[...], w_value[...], preferred_element_type=F32).astype(BF16)
        queries = jnp.dot(x[: 2 * BLOCK, :], w_query[...], preferred_element_type=F32).astype(BF16) * scale
        lane = lax.broadcasted_iota(jnp.int32, (BLOCK, 128), 1)
        v = values[...]
        for b in range(2):
            here = slice(b * BLOCK, (b + 1) * BLOCK)
            scores = lax.dot_general(spread_heads(queries[here], head_dim), keys[...], NT, preferred_element_type=F32)
            top = jnp.max(scores, axis=1, keepdims=True)
            expo = jnp.exp(scores - top)
            total = jnp.sum(expo, axis=1, keepdims=True)
            high_part = expo.astype(BF16)
            low_part = (expo - high_part.astype(F32)).astype(BF16)
            wide = jnp.dot(high_part, v, preferred_element_type=F32) + jnp.dot(
                low_part, v, preferred_element_type=F32
            )
            part[here, :lanes] = fold_heads(wide * (1.0 / total), head_dim)
            level = top + jnp.log(total)
            levels = jnp.zeros((BLOCK, 128), F32)
            for j in range(GROUP):
                levels = jnp.where(lane == j, level[j * BLOCK : (j + 1) * BLOCK], levels)
            part[here, lanes:] = levels

    return near_kernel


def near_projection(lay, table, half, theirs, low, high, weights, keys, values):
    rows, width = keys.shape
    lanes = width * GROUP // HEADS
    column = lambda g: (0, g)
    return pl.pallas_call(
        make_near(lay),
        grid=(width // lanes,),
        out_shape=[hbm_out((4 * BLOCK, width), BF16)] * 2
        + [hbm_out((2 * BLOCK, width // lanes * (lanes + 128)), F32)],
        in_specs=[whole(pltpu.SMEM)]
        + [pl.BlockSpec((BLOCK, width), lambda g: (0, 0))] * 4
        + [pl.BlockSpec((width, lanes), column)] * 3
        + [pl.BlockSpec((rows, lanes), column)] * 2,
        out_specs=[pl.BlockSpec((4 * BLOCK, lanes), column)] * 2 + [pl.BlockSpec((2 * BLOCK, lanes + 128), column)],
        scratch_shapes=[pltpu.VMEM((4 * BLOCK, width), BF16)],
        compiler_params=pltpu.CompilerParams(vmem_limit_bytes=20 << 20),
    )(table, *in_hbm(half, theirs, low, high, *weights, keys, values))


def join_parts(parts, w_out, devices):
    share = parts.shape[0] // devices
    width = w_out.shape[0]
    lanes = width * GROUP // HEADS
    head_dim = lanes // GROUP

    def kernel(parts, w_out, out):
        pieces = []
        for g in range(HEADS // GROUP):
            base = g * (lanes + 128)
            levels = [parts[d * share : (d + 1) * share, base + lanes : base + lanes + 128] for d in range(devices)]
            top = levels[0]
            for level in levels[1:]:
                top = jnp.maximum(top, level)
            factors = [jnp.exp(level - top) for level in levels]
            total = factors[0]
            for f in factors[1:]:
                total = total + f
            inverse = 1.0 / total
            which = lane_head((share, lanes), head_dim)
            joined = jnp.zeros((share, lanes), F32)
            for d in range(devices):
                f = factors[d] * inverse
                spread = jnp.broadcast_to(f[:, 0:1], (share, lanes))
                for j in range(1, GROUP):
                    spread = jnp.where(which == j, f[:, j : j + 1], spread)
                joined = joined + parts[d * share : (d + 1) * share, base : base + lanes] * spread
            pieces.append(joined.astype(BF16))
        full = jnp.concatenate(pieces, axis=1)
        done = jnp.dot(full, w_out[...], preferred_element_type=F32)
        out[...] = jnp.concatenate([done] * devices, axis=0).astype(BF16)

    return pl.pallas_call(
        kernel,
        grid=(1,),
        out_shape=hbm_out((devices * share, width), BF16),
        in_specs=[pl.BlockSpec(a.shape, lambda i: (0, 0)) for a in (parts, w_out)],
        out_specs=pl.BlockSpec((devices * share, width), lambda i: (0, 0)),
        compiler_params=pltpu.CompilerParams(vmem_limit_bytes=20 << 20),
    )(*in_hbm(parts, w_out))


def attend(queries, keys, values, near_k, near_v, other, w_out):
    rows, width = queries.shape
    blocks = rows // BLOCK
    head_dim = width // HEADS
    lanes = GROUP * head_dim
    listed = 3 * BLOCK

    def kernel(queries, keys, values, near_k, near_v, other, from_out, out, mixed, w_out, sem):
        i = pl.program_id(0)
        load = pltpu.make_async_copy(from_out, w_out, sem.at[0])

        @pl.when(i == 0)
        def _():
            load.start()

        last = blocks - 1
        here = rows_at(i)

        def window(own, near, cols):
            before = own[rows_at(jnp.maximum(i - 1, 0)), cols]
            after = own[rows_at(jnp.minimum(i + 1, last)), cols]
            before = jnp.where(i == 0, near[2 * BLOCK : 3 * BLOCK, cols], before)
            after = jnp.where(i == last, near[3 * BLOCK : 4 * BLOCK, cols], after)
            return [before, own[here, cols], after, near[: 2 * BLOCK, cols]]

        for g in range(HEADS // GROUP):
            cols = slice(g * lanes, (g + 1) * lanes)
            q = spread_heads(queries[:, cols], head_dim)
            k = jnp.concatenate(window(keys, near_k, cols) + [other[:, cols]], axis=0)
            v = jnp.concatenate(window(values, near_v, cols) + [other[:, width + g * lanes : width + (g + 1) * lanes]], axis=0)
            scores = lax.dot_general(q, k, NT, preferred_element_type=F32)
            top = jnp.max(scores, axis=1, keepdims=True)
            expo = jnp.exp(scores - top)
            total = jnp.sum(expo, axis=1, keepdims=True)
            weights = (expo * (1.0 / total)).astype(BF16)
            wide = jnp.dot(weights, v, preferred_element_type=F32)
            mixed[here, cols] = fold_heads(wide, head_dim).astype(BF16)

        @pl.when(i == last)
        def _():
            load.wait()
            out[...] = jnp.dot(mixed[...], w_out[...], preferred_element_type=F32).astype(BF16)

    return pl.pallas_call(
        kernel,
        grid=(blocks,),
        out_shape=hbm_out((rows, width), BF16),
        in_specs=[pl.BlockSpec((BLOCK, width), lambda i: (i, 0))]
        + [pl.BlockSpec(a.shape, lambda i: (0, 0)) for a in (keys, values, near_k, near_v)]
        + [pl.BlockSpec((listed, 2 * width), lambda i: (i, 0)), whole(pltpu.HBM)],
        out_specs=pl.BlockSpec((rows, width), lambda i: (0, 0)),
        scratch_shapes=[
            pltpu.VMEM((rows, width), BF16),
            pltpu.VMEM(w_out.shape, BF16),
            pltpu.SemaphoreType.DMA((1,)),
        ],
        compiler_params=pltpu.CompilerParams(vmem_limit_bytes=32 << 20),
    )(*in_hbm(queries, keys, values, near_k, near_v, other, w_out))


def put_fixed(lay, table, fixed, out):
    def kernel(table, fixed, before, out, sem):
        for j in range(2):

            @pl.when(table[lay.own + 2 * j] == 1)
            def _():
                to = rows_at(table[lay.own + 2 * j + 1])
                start_all(
                    [pltpu.make_async_copy(fixed.at[pl.ds(j * BLOCK, BLOCK), :], out.at[to, :], sem.at[j])]
                )

    return pl.pallas_call(
        kernel,
        out_shape=hbm_out(out.shape, out.dtype),
        in_specs=[whole(pltpu.SMEM), whole(pltpu.HBM), whole(pltpu.HBM)],
        out_specs=whole(pltpu.HBM),
        scratch_shapes=[pltpu.SemaphoreType.DMA((2,))],
        input_output_aliases={2: 0},
    )(table, *in_hbm(fixed, out))


def together(*arrays):
    return lax.optimization_barrier(arrays)


def on_device(tokens, w_query, w_key, w_value, w_out, rand_table, global_blocks):
    rows, width = tokens.shape
    blocks = rows // BLOCK
    devices = lax.axis_size("seq")
    myself = lax.axis_index("seq")
    lay = Layout(devices, blocks)
    weights = (w_query, w_key, w_value)

    def send(array, pairs):
        return lax.ppermute(array, "seq", pairs)

    def swap(array, bit):
        return send(array, [(i, i ^ bit) for i in range(devices)])

    me = myself.reshape(1).astype(jnp.int32)
    core = myself % 2

    pair = owned_pair(lay, me, global_blocks, tokens)
    edge_before = send(tokens[rows - BLOCK :], [(i, (i + 1) % devices) for i in range(devices)])
    edge_after = send(tokens[:BLOCK], [((i + 1) % devices, i) for i in range(devices)])
    pair = pair + swap(pair, 1)
    half = jnp.where(core == 0, pair[:BLOCK], pair[BLOCK:])
    high_bits = [4 << b for b in range(lay.tall.bit_length() - 1)]
    for bit in high_bits:
        half = half + swap(half, bit)
    early, half, edge_before, edge_after = together(tokens, half, edge_before, edge_after)
    sets = {bit >> 2: swap(early, bit) for bit in high_bits}
    half = half + swap(half, 2)
    theirs = swap(half, 1)
    table = make_route(lay)(me, rand_table, global_blocks)

    def ask(array, picked):
        return [array] + [swap(m, t + 1) for t, m in enumerate(picked)]

    queries, keys, values = local_projection(tokens, weights)
    near_k, near_v, part = near_projection(
        lay, table, half, theirs, edge_before, edge_after, weights, keys, values
    )
    def project(which, set_and_messages, kv):
        return project_stages(lay, 1 + which, 1 + which, table, [set_and_messages], w_key, w_value, kv)

    waiting = (0, ask(tokens, pick(lay, 0, table, tokens)))
    arrivals = []
    for bit in reversed(high_bits):
        arrivals += [bit >> 2 | w for w in [0] + arrivals]
    other = parts = None
    for count, w in enumerate(arrivals):
        if count == 0:
            direct = sorted(sets)
            joint = together(*waiting[1], *(sets[d] for d in direct))
            waiting = (0, joint[:4])
            sets.update(zip(direct, joint[4:]))
        else:
            sets[w], other = together(sets[w], other)
        for later in range(1, lay.tall):
            low = later & -later
            if later ^ low == w:
                sets[later] = swap(sets[w], low << 2)
        picked = pick(lay, w, table, sets[w])
        if count == 0:
            *picked, part = together(*picked, part)
            parts = lax.all_to_all(part, "seq", 0, 0, tiled=True)
        which, held = waiting
        held = together(*held, *picked)[:4]
        other = project(which, held, other)
        waiting = (w, ask(sets[w], picked))
    joined = join_parts(parts, w_out, devices)
    which, held = waiting
    fixed = lax.all_to_all(joined, "seq", 0, 0, tiled=True)
    *held, other, _ = together(*held, other, joined)
    other = project(which, held, other)

    out = attend(queries, keys, values, near_k, near_v, other, w_out)
    return put_fixed(lay, table, fixed, out)


def solution(mesh):
    in_specs = (P(("groups", "seq"), None), P(), P(), P(), P(), P(), P())
    out_specs = P(("groups", "seq"), None)
    return jax.shard_map(
        on_device, mesh=mesh, in_specs=in_specs, out_specs=out_specs, check_vma=False
    )
```

```python
import math

import jax
import jax.numpy as jnp
from jax import lax
from jax.experimental import pallas as pl
from jax.experimental.pallas import tpu as pltpu
from jax.sharding import PartitionSpec as P

HEADS = 16
BLOCK = 64
GROUP = 4
CHUNK = 8
TURNS = 2
NT = (((1,), (1,)), ((), ()))
BF16 = jnp.bfloat16
F32 = jnp.float32


def in_hbm(*arrays):
    return [pltpu.with_memory_space_constraint(a, pltpu.HBM) for a in arrays]


def hbm_out(shape, dtype):
    return pltpu.HBM(shape, dtype)


def whole(memory=pltpu.VMEM):
    return pl.BlockSpec(memory_space=memory)


def rows_at(block, count=1):
    return pl.ds(pl.multiple_of(block * BLOCK, BLOCK), count * BLOCK)


def lane_head(shape, head_dim):
    return lax.broadcasted_iota(jnp.int32, shape, 1) // head_dim


def spread_heads(q, head_dim):
    which = lane_head(q.shape, head_dim)
    zero = jnp.zeros_like(q)
    return jnp.concatenate([jnp.where(which == j, q, zero) for j in range(GROUP)], axis=0)


def fold_heads(wide, head_dim):
    rows = wide.shape[0] // GROUP
    which = lane_head((rows, wide.shape[1]), head_dim)
    out = wide[:rows]
    for j in range(1, GROUP):
        out = jnp.where(which == j, wide[j * rows : (j + 1) * rows], out)
    return out


class Layout:
    def __init__(self, devices, blocks):
        self.devices, self.blocks = devices, blocks
        self.tall = devices // 4
        self.slots = 3 * blocks
        self.caps = -(-self.slots // devices) + 1
        self.asked = 0
        self.bounds = self.asked + self.tall * 3 * self.caps
        self.order = self.bounds + self.tall + 2
        self.source = self.order + self.slots
        self.index = self.source + self.slots
        self.own = self.index + self.slots
        self.core = self.own + 4
        self.spare = self.core + 1
        self.size = self.spare + 1


def make_route(lay):
    devices, blocks, tall, slots, caps = lay.devices, lay.blocks, lay.tall, lay.slots, lay.caps
    power = blocks.bit_length() - 1
    assert blocks == 1 << power and tall & (tall - 1) == 0

    def route_kernel(me, table, global_blocks, out, seen, stages, filled):
        myself = me[0]
        zero = jnp.int32(0)

        for i in range(tall * 3 * caps):
            out[lay.asked + i] = zero

        for t in range(1, 4):
            for w in range(tall):
                filled[w] = zero

            def asks(i, carry):
                for u in range(3):
                    block = table[(myself ^ t) * blocks + i, u]
                    apart = (block >> power) ^ myself
                    fits = (apart & 3) == 0
                    which = apart >> 2
                    rank = filled[which]
                    filled[which] = rank + fits.astype(jnp.int32)
                    at = lay.asked + (which * 3 + t - 1) * caps + rank
                    out[jnp.where(fits, at, lay.spare)] = block & (blocks - 1)
                return carry

            lax.fori_loop(0, blocks, asks, 0)

        for o in range(devices):
            seen[o] = zero
        for g in range(tall + 2):
            filled[g] = zero

        def mine(i, carry):
            for u in range(3):
                block = table[myself * blocks + i, u]
                owner = block >> power
                local = block & (blocks - 1)
                rank = seen[owner]
                seen[owner] = rank + 1
                s = i * 3 + u
                apart = owner ^ myself
                stage = 1 + (apart >> 2)
                source = apart & 3
                out[lay.source + s] = source
                out[lay.index + s] = jnp.where(source == 0, local, rank)
                stages[s] = stage
                filled[stage] = filled[stage] + 1
            return carry

        lax.fori_loop(0, blocks, mine, 0)
        start = zero
        for g in range(tall + 2):
            out[lay.bounds + g] = start
            if g < tall + 1:
                now = filled[g]
                filled[g] = start
                start = start + now

        def put(s, carry):
            stage = stages[s]
            at = filled[stage]
            filled[stage] = at + 1
            out[lay.order + at] = s
            return carry

        lax.fori_loop(0, slots, put, 0)
        for j in range(2):
            g = global_blocks[j]
            out[lay.own + 2 * j] = ((g >> power) == myself).astype(jnp.int32)
            out[lay.own + 2 * j + 1] = g & (blocks - 1)
        out[lay.core] = myself & 1
        out[lay.spare] = zero

    return pl.pallas_call(
        route_kernel,
        out_shape=jax.ShapeDtypeStruct((lay.size,), jnp.int32),
        in_specs=[whole(pltpu.SMEM)] * 3,
        out_specs=whole(pltpu.SMEM),
        scratch_shapes=[
            pltpu.SMEM((devices,), jnp.int32),
            pltpu.SMEM((slots,), jnp.int32),
            pltpu.SMEM((tall + 2,), jnp.int32),
        ],
    )


def start_all(copies):
    for c in copies:
        c.start()
    for c in copies:
        c.wait()


def owned_pair(lay, me, global_blocks, tokens):
    blocks = lay.blocks

    def kernel(me, global_blocks, tokens, pair, sem):
        start_all(
            [
                pltpu.make_async_copy(
                    tokens.at[rows_at(global_blocks[j] % blocks), :], pair.at[pl.ds(j * BLOCK, BLOCK), :], sem.at[j]
                )
                for j in range(2)
            ]
        )
        for j in range(2):

            @pl.when(global_blocks[j] // blocks != me[0])
            def _():
                pair[j * BLOCK : (j + 1) * BLOCK, :] = jnp.zeros((BLOCK, pair.shape[1]), BF16)

    return pl.pallas_call(
        kernel,
        out_shape=jax.ShapeDtypeStruct((2 * BLOCK, tokens.shape[1]), BF16),
        in_specs=[whole(pltpu.SMEM)] * 2 + [whole(pltpu.HBM)],
        out_specs=whole(),
        scratch_shapes=[pltpu.SemaphoreType.DMA((2,))],
    )(me, global_blocks, *in_hbm(tokens))


def pick(lay, which, table, tokens):
    caps = lay.caps
    base = lay.asked + which * 3 * caps

    def kernel(table, tokens, *refs):
        outs, rows, sem_in, sem_out = refs[:3], refs[3], refs[4], refs[5]
        gets = [
            pltpu.make_async_copy(
                tokens.at[rows_at(table[base + i]), :], rows.at[pl.ds(i * BLOCK, BLOCK), :], sem_in.at[i]
            )
            for i in range(3 * caps)
        ]
        puts = [
            pltpu.make_async_copy(rows.at[pl.ds(t * caps * BLOCK, caps * BLOCK), :], outs[t], sem_out.at[t])
            for t in range(3)
        ]
        for c in gets:
            c.start()
        for t in range(3):
            for c in gets[t * caps : (t + 1) * caps]:
                c.wait()
            puts[t].start()
        for c in puts:
            c.wait()

    return pl.pallas_call(
        kernel,
        out_shape=[hbm_out((caps * BLOCK, tokens.shape[1]), BF16)] * 3,
        in_specs=[whole(pltpu.SMEM), whole(pltpu.HBM)],
        out_specs=[whole(pltpu.HBM)] * 3,
        scratch_shapes=[
            pltpu.VMEM((3 * caps * BLOCK, tokens.shape[1]), BF16),
            pltpu.SemaphoreType.DMA((3 * caps,)),
            pltpu.SemaphoreType.DMA((3,)),
        ],
    )(table, *in_hbm(tokens))


def project_stages(lay, first_stage, last_stage, table, sets, w_key, w_value, kv):
    flat = [array for arrays in sets for array in arrays]

    def kernel(table, *refs):
        arrived, from_key, from_value = refs[: len(flat)], refs[len(flat)], refs[len(flat) + 1]
        out, w_key, w_value, rows, made, sem_w, sem_in, sem_out = refs[-8:]
        width = w_key.shape[1]
        loads = [
            pltpu.make_async_copy(from_key, w_key, sem_w.at[0]),
            pltpu.make_async_copy(from_value, w_value, sem_w.at[1]),
        ]
        for c in loads:
            c.start()
        low = table[lay.bounds + first_stage]
        high = table[lay.bounds + last_stage + 1]

        def one_chunk(c, carry):
            first = low + c * CHUNK

            def get(j, ref, here):
                return pltpu.make_async_copy(ref.at[here, :], rows.at[pl.ds(j * BLOCK, BLOCK), :], sem_in.at[j])

            def fetch(j):
                e = table[lay.order + first + j]
                here = rows_at(table[lay.index + e])
                source = table[lay.source + e]
                for i in range(len(sets)):
                    stage = first_stage + i
                    inside = (first + j >= table[lay.bounds + stage]) & (first + j < table[lay.bounds + stage + 1])
                    for t in range(4):

                        @pl.when(inside & (source == t))
                        def _():
                            get(j, arrived[4 * i + t], here).start()

            def put(j):
                to = rows_at(table[lay.order + first + j])
                return pltpu.make_async_copy(made.at[pl.ds(j * BLOCK, BLOCK), :], out.at[to, :], sem_out.at[j])

            def each(action):
                for j in range(CHUNK):

                    @pl.when(first + j < high)
                    def _():
                        action(j)

            each(fetch)
            each(lambda j: get(j, arrived[0], pl.ds(0, BLOCK)).wait())

            @pl.when(c == 0)
            def _():
                for load in loads:
                    load.wait()

            made[:, :width] = jnp.dot(rows[...], w_key[...], preferred_element_type=F32).astype(BF16)
            made[:, width:] = jnp.dot(rows[...], w_value[...], preferred_element_type=F32).astype(BF16)
            each(lambda j: put(j).start())
            each(lambda j: put(j).wait())
            return carry

        lax.fori_loop(0, (high - low + CHUNK - 1) // CHUNK, one_chunk, 0)

        @pl.when(high == low)
        def _():
            for load in loads:
                load.wait()

    width = w_key.shape[1]
    arrays = [table] + flat + [w_key, w_value]
    specs = [whole(pltpu.SMEM)] + [whole(pltpu.HBM)] * (len(flat) + 2)
    aliases = {}
    if kv is not None:
        aliases = {len(arrays): 0}
        arrays.append(kv)
        specs.append(whole(pltpu.HBM))
    return pl.pallas_call(
        kernel,
        out_shape=hbm_out((lay.slots * BLOCK, 2 * width), BF16),
        in_specs=specs,
        out_specs=whole(pltpu.HBM),
        scratch_shapes=[
            pltpu.VMEM((width, width), BF16),
            pltpu.VMEM((width, width), BF16),
            pltpu.VMEM((CHUNK * BLOCK, width), BF16),
            pltpu.VMEM((CHUNK * BLOCK, 2 * width), BF16),
            pltpu.SemaphoreType.DMA((2,)),
            pltpu.SemaphoreType.DMA((CHUNK,)),
            pltpu.SemaphoreType.DMA((CHUNK,)),
        ],
        input_output_aliases=aliases,
        compiler_params=pltpu.CompilerParams(vmem_limit_bytes=24 << 20),
    )(arrays[0], *in_hbm(*arrays[1:]))


def local_kernel(tokens, w_query, w_key, w_value, queries, keys, values):
    scale = jnp.asarray(1.0 / math.sqrt(queries.shape[1] // GROUP), BF16)
    x = tokens[...]
    queries[...] = jnp.dot(x, w_query[...], preferred_element_type=F32).astype(BF16) * scale
    keys[...] = jnp.dot(x, w_key[...], preferred_element_type=F32).astype(BF16)
    values[...] = jnp.dot(x, w_value[...], preferred_element_type=F32).astype(BF16)


def local_projection(tokens, weights):
    rows, width = tokens.shape
    lanes = width * GROUP // HEADS
    column = lambda g: (0, g)
    return pl.pallas_call(
        local_kernel,
        grid=(width // lanes,),
        out_shape=[hbm_out((rows, width), BF16)] * 3,
        in_specs=[pl.BlockSpec((rows, width), lambda g: (0, 0))] + [pl.BlockSpec((width, lanes), column)] * 3,
        out_specs=[pl.BlockSpec((rows, lanes), column)] * 3,
        compiler_params=pltpu.CompilerParams(vmem_limit_bytes=20 << 20),
    )(*in_hbm(tokens, *weights))


def make_near(lay):
    def near_kernel(table, half, theirs, low, high, w_query, w_key, w_value, keys, values, near_k, near_v, part, x):
        lanes = keys.shape[1]
        head_dim = lanes // GROUP
        scale = jnp.asarray(1.0 / math.sqrt(head_dim), BF16)

        @pl.when(pl.program_id(0) == 0)
        def _():
            x[2 * BLOCK : 3 * BLOCK, :] = low[...]
            x[3 * BLOCK :, :] = high[...]

            @pl.when(table[lay.core] == 0)
            def _():
                x[:BLOCK, :] = half[...]
                x[BLOCK : 2 * BLOCK, :] = theirs[...]

            @pl.when(table[lay.core] == 1)
            def _():
                x[:BLOCK, :] = theirs[...]
                x[BLOCK : 2 * BLOCK, :] = half[...]

        near_k[...] = jnp.dot(x[...], w_key[...], preferred_element_type=F32).astype(BF16)
        near_v[...] = jnp.dot(x[...], w_value[...], preferred_element_type=F32).astype(BF16)
        queries = jnp.dot(x[: 2 * BLOCK, :], w_query[...], preferred_element_type=F32).astype(BF16) * scale
        lane = lax.broadcasted_iota(jnp.int32, (BLOCK, 128), 1)
        v = values[...]
        for b in range(2):
            here = slice(b * BLOCK, (b + 1) * BLOCK)
            scores = lax.dot_general(spread_heads(queries[here], head_dim), keys[...], NT, preferred_element_type=F32)
            top = jnp.max(scores, axis=1, keepdims=True)
            expo = jnp.exp(scores - top)
            total = jnp.sum(expo, axis=1, keepdims=True)
            high_part = expo.astype(BF16)
            low_part = (expo - high_part.astype(F32)).astype(BF16)
            wide = jnp.dot(high_part, v, preferred_element_type=F32) + jnp.dot(
                low_part, v, preferred_element_type=F32
            )
            part[here, :lanes] = fold_heads(wide * (1.0 / total), head_dim)
            level = top + jnp.log(total)
            levels = jnp.zeros((BLOCK, 128), F32)
            for j in range(GROUP):
                levels = jnp.where(lane == j, level[j * BLOCK : (j + 1) * BLOCK], levels)
            part[here, lanes:] = levels

    return near_kernel


def near_projection(lay, table, half, theirs, low, high, weights, keys, values):
    rows, width = keys.shape
    lanes = width * GROUP // HEADS
    column = lambda g: (0, g)
    return pl.pallas_call(
        make_near(lay),
        grid=(width // lanes,),
        out_shape=[hbm_out((4 * BLOCK, width), BF16)] * 2
        + [hbm_out((2 * BLOCK, width // lanes * (lanes + 128)), F32)],
        in_specs=[whole(pltpu.SMEM)]
        + [pl.BlockSpec((BLOCK, width), lambda g: (0, 0))] * 4
        + [pl.BlockSpec((width, lanes), column)] * 3
        + [pl.BlockSpec((rows, lanes), column)] * 2,
        out_specs=[pl.BlockSpec((4 * BLOCK, lanes), column)] * 2 + [pl.BlockSpec((2 * BLOCK, lanes + 128), column)],
        scratch_shapes=[pltpu.VMEM((4 * BLOCK, width), BF16)],
        compiler_params=pltpu.CompilerParams(vmem_limit_bytes=20 << 20),
    )(table, *in_hbm(half, theirs, low, high, *weights, keys, values))


def join_parts(parts, w_out, devices):
    share = parts.shape[0] // devices
    width = w_out.shape[0]
    lanes = width * GROUP // HEADS
    head_dim = lanes // GROUP

    def kernel(parts, w_out, out):
        pieces = []
        for g in range(HEADS // GROUP):
            base = g * (lanes + 128)
            levels = [parts[d * share : (d + 1) * share, base + lanes : base + lanes + 128] for d in range(devices)]
            top = levels[0]
            for level in levels[1:]:
                top = jnp.maximum(top, level)
            factors = [jnp.exp(level - top) for level in levels]
            total = factors[0]
            for f in factors[1:]:
                total = total + f
            inverse = 1.0 / total
            which = lane_head((share, lanes), head_dim)
            joined = jnp.zeros((share, lanes), F32)
            for d in range(devices):
                f = factors[d] * inverse
                spread = jnp.broadcast_to(f[:, 0:1], (share, lanes))
                for j in range(1, GROUP):
                    spread = jnp.where(which == j, f[:, j : j + 1], spread)
                joined = joined + parts[d * share : (d + 1) * share, base : base + lanes] * spread
            pieces.append(joined.astype(BF16))
        full = jnp.concatenate(pieces, axis=1)
        done = jnp.dot(full, w_out[...], preferred_element_type=F32)
        out[...] = jnp.concatenate([done] * devices, axis=0).astype(BF16)

    return pl.pallas_call(
        kernel,
        grid=(1,),
        out_shape=hbm_out((devices * share, width), BF16),
        in_specs=[pl.BlockSpec(a.shape, lambda i: (0, 0)) for a in (parts, w_out)],
        out_specs=pl.BlockSpec((devices * share, width), lambda i: (0, 0)),
        compiler_params=pltpu.CompilerParams(vmem_limit_bytes=20 << 20),
    )(*in_hbm(parts, w_out))


def attend(queries, keys, values, near_k, near_v, other, w_out):
    rows, width = queries.shape
    blocks = rows // BLOCK
    head_dim = width // HEADS
    lanes = GROUP * head_dim
    listed = 3 * BLOCK

    def kernel(queries, keys, values, near_k, near_v, other, from_out, out, mixed, w_out, sem):
        load = pltpu.make_async_copy(from_out, w_out, sem.at[0])

        @pl.when(pl.program_id(0) == 0)
        def _():
            load.start()

        last = blocks - 1

        def window(i, own, near, cols):
            before = own[rows_at(jnp.maximum(i - 1, 0)), cols]
            after = own[rows_at(jnp.minimum(i + 1, last)), cols]
            before = jnp.where(i == 0, near[2 * BLOCK : 3 * BLOCK, cols], before)
            after = jnp.where(i == last, near[3 * BLOCK : 4 * BLOCK, cols], after)
            return [before, own[rows_at(i), cols], after, near[: 2 * BLOCK, cols]]

        for turn in range(TURNS):
            i = pl.program_id(0) * TURNS + turn
            here = rows_at(i)
            mine = slice(turn * BLOCK, (turn + 1) * BLOCK)
            theirs = slice(turn * listed, (turn + 1) * listed)
            for g in range(HEADS // GROUP):
                cols = slice(g * lanes, (g + 1) * lanes)
                more = slice(width + g * lanes, width + (g + 1) * lanes)
                q = spread_heads(queries[mine, cols], head_dim)
                k = jnp.concatenate(window(i, keys, near_k, cols) + [other[theirs, cols]], axis=0)
                v = jnp.concatenate(window(i, values, near_v, cols) + [other[theirs, more]], axis=0)
                scores = lax.dot_general(q, k, NT, preferred_element_type=F32)
                top = jnp.max(scores, axis=1, keepdims=True)
                expo = jnp.exp(scores - top)
                total = jnp.sum(expo, axis=1, keepdims=True)
                weights = (expo * (1.0 / total)).astype(BF16)
                wide = jnp.dot(weights, v, preferred_element_type=F32)
                mixed[here, cols] = fold_heads(wide, head_dim).astype(BF16)

        @pl.when(pl.program_id(0) == pl.num_programs(0) - 1)
        def _():
            load.wait()
            out[...] = jnp.dot(mixed[...], w_out[...], preferred_element_type=F32).astype(BF16)

    return pl.pallas_call(
        kernel,
        grid=(blocks // TURNS,),
        out_shape=hbm_out((rows, width), BF16),
        in_specs=[pl.BlockSpec((TURNS * BLOCK, width), lambda i: (i, 0))]
        + [pl.BlockSpec(a.shape, lambda i: (0, 0)) for a in (keys, values, near_k, near_v)]
        + [pl.BlockSpec((TURNS * listed, 2 * width), lambda i: (i, 0)), whole(pltpu.HBM)],
        out_specs=pl.BlockSpec((rows, width), lambda i: (0, 0)),
        scratch_shapes=[
            pltpu.VMEM((rows, width), BF16),
            pltpu.VMEM(w_out.shape, BF16),
            pltpu.SemaphoreType.DMA((1,)),
        ],
        compiler_params=pltpu.CompilerParams(vmem_limit_bytes=32 << 20),
    )(*in_hbm(queries, keys, values, near_k, near_v, other, w_out))


def put_fixed(lay, table, fixed, out):
    def kernel(table, fixed, before, out, sem):
        for j in range(2):

            @pl.when(table[lay.own + 2 * j] == 1)
            def _():
                to = rows_at(table[lay.own + 2 * j + 1])
                start_all(
                    [pltpu.make_async_copy(fixed.at[pl.ds(j * BLOCK, BLOCK), :], out.at[to, :], sem.at[j])]
                )

    return pl.pallas_call(
        kernel,
        out_shape=hbm_out(out.shape, out.dtype),
        in_specs=[whole(pltpu.SMEM), whole(pltpu.HBM), whole(pltpu.HBM)],
        out_specs=whole(pltpu.HBM),
        scratch_shapes=[pltpu.SemaphoreType.DMA((2,))],
        input_output_aliases={2: 0},
    )(table, *in_hbm(fixed, out))


def together(*arrays):
    return lax.optimization_barrier(arrays)


def on_device(tokens, w_query, w_key, w_value, w_out, rand_table, global_blocks):
    rows, width = tokens.shape
    blocks = rows // BLOCK
    devices = lax.axis_size("seq")
    myself = lax.axis_index("seq")
    lay = Layout(devices, blocks)
    weights = (w_query, w_key, w_value)

    def send(array, pairs):
        return lax.ppermute(array, "seq", pairs)

    def swap(array, bit):
        return send(array, [(i, i ^ bit) for i in range(devices)])

    me = myself.reshape(1).astype(jnp.int32)
    core = myself % 2

    pair = owned_pair(lay, me, global_blocks, tokens)
    edge_before = send(tokens[rows - BLOCK :], [(i, (i + 1) % devices) for i in range(devices)])
    edge_after = send(tokens[:BLOCK], [((i + 1) % devices, i) for i in range(devices)])
    pair = pair + swap(pair, 1)
    half = jnp.where(core == 0, pair[:BLOCK], pair[BLOCK:])
    high_bits = [4 << b for b in range(lay.tall.bit_length() - 1)]
    for bit in high_bits:
        half = half + swap(half, bit)
    early, half, edge_before, edge_after = together(tokens, half, edge_before, edge_after)
    sets = {bit >> 2: swap(early, bit) for bit in high_bits}
    half = half + swap(half, 2)
    theirs = swap(half, 1)
    table = make_route(lay)(me, rand_table, global_blocks)

    def ask(array, picked):
        return [array] + [swap(m, t + 1) for t, m in enumerate(picked)]

    queries, keys, values = local_projection(tokens, weights)
    near_k, near_v, part = near_projection(
        lay, table, half, theirs, edge_before, edge_after, weights, keys, values
    )
    def project(which, set_and_messages, kv):
        return project_stages(lay, 1 + which, 1 + which, table, [set_and_messages], w_key, w_value, kv)

    waiting = (0, ask(tokens, pick(lay, 0, table, tokens)))
    arrivals = []
    for bit in reversed(high_bits):
        arrivals += [bit >> 2 | w for w in [0] + arrivals]
    other = parts = None
    for count, w in enumerate(arrivals):
        if count == 0:
            direct = sorted(sets)
            joint = together(*waiting[1], *(sets[d] for d in direct))
            waiting = (0, joint[:4])
            sets.update(zip(direct, joint[4:]))
        else:
            sets[w], other = together(sets[w], other)
        for later in range(1, lay.tall):
            low = later & -later
            if later ^ low == w:
                sets[later] = swap(sets[w], low << 2)
        picked = pick(lay, w, table, sets[w])
        if count == 0:
            *picked, part = together(*picked, part)
            parts = lax.all_to_all(part, "seq", 0, 0, tiled=True)
        which, held = waiting
        held = together(*held, *picked)[:4]
        other = project(which, held, other)
        waiting = (w, ask(sets[w], picked))
    joined = join_parts(parts, w_out, devices)
    which, held = waiting
    fixed = lax.all_to_all(joined, "seq", 0, 0, tiled=True)
    *held, other, _ = together(*held, other, joined)
    other = project(which, held, other)

    out = attend(queries, keys, values, near_k, near_v, other, w_out)
    return put_fixed(lay, table, fixed, out)


def solution(mesh):
    in_specs = (P(("groups", "seq"), None), P(), P(), P(), P(), P(), P())
    out_specs = P(("groups", "seq"), None)
    return jax.shard_map(
        on_device, mesh=mesh, in_specs=in_specs, out_specs=out_specs, check_vma=False
    )
```
